256 devices in a mesh: seq: 32 (over x, y, core), head: 8 (over z).
Axes of the slice: x: 4, y: 4, z: 8, core: 2. Of those that a mesh axis runs over, the one named last changes fastest.
Arguments:
- new_states: bfloat16 [96, 1024], replicated, may hold values from -6 to 6
- lengths: int32 [24], replicated, may hold values from 1 to 16380, as said below
- cache_keys: bfloat16 [24, 16384, 1024], P(None, 'seq', 'head'), may hold values from -3000 to 3000
- cache_values: bfloat16 [24, 16384, 1024], P(None, 'seq', 'head'), may hold values from -6 to 6
- buckets: int32 [24, 4, 16384], P(None, None, 'seq'), may hold values from 0 to 31, as said below
- attn_gain: float32 [1024], replicated, may hold values from 0.25 to 1.75
- w_query: bfloat16 [1024, 1024], P(None, 'head'), may hold values from -0.0234375 to 0.0234375
- w_key: bfloat16 [1024, 1024], P(None, 'head'), may hold values from -0.1875 to 0.1875
- w_value: bfloat16 [1024, 1024], P(None, 'head'), may hold values from -0.1875 to 0.1875
- rel_bias: float32 [32, 16], P(None, 'head'), may hold values from -27 to 2
- w_out: bfloat16 [1024, 1024], P('head'), may hold values from -0.1875 to 0.1875
- ffn_gain: float32 [1024], replicated, may hold values from 0.25 to 1.75
- w_router: float32 [1024, 16], replicated, may hold values from -0.1875 to 0.1875
- w_gate: bfloat16 [16, 1024, 2816], P('head', None, 'seq'), may hold values from -0.1875 to 0.1875
- w_up: bfloat16 [16, 1024, 2816], P('head', None, 'seq'), may hold values from -0.1875 to 0.1875
- w_down: bfloat16 [16, 2816, 1024], P('head', 'seq'), may hold values from -0.109375 to 0.109375
- expert_picks: int32 [4, 24, 2], replicated, may hold values from 0 to 15, all different within a row; in each aligned block of 24 rows (0 to 23, 24 to 47, ..., all dimensions but the last counted through in order) at most 4 rows name the same one
- final_gain: float32 [1024], replicated, may hold values from 0.25 to 1.75
- w_vocab: bfloat16 [1024, 32128], P(None, 'seq'), may hold values from -0.5 to 0.5
Outputs:
- final_hidden: bfloat16 [96, 1024], P('head')
- hidden_norm: float32 [96], P('head')
- logit_max: float32 [96], P('head')
The draws below stay inside these ranges and needn't reach their ends.
Inputs may be any that keep to these rules, and one draw needn't show every extreme that they name: `lengths`: some request has exactly 16380 cached positions. buckets[r, t, p] is the T5 relative position bucket (16 exact buckets, then logarithmic up to a distance of 128) of the distance lengths[r] + t - p where that is not negative, else 0. `expert_picks`: A request's two picks at a step differ; at each step no expert is picked by more than 4 requests, a bound that some block reaches.
All inputs are finite; a program needn't handle non-finite values.
Results may differ from the reference program's by a relative error of at most 0.0096.
Values may be sent and summed in bfloat16 or wider, within the bound.
A program may use at most 64 MiB of HBM per device.

```python
import math
import jax
import jax.numpy as jnp
import numpy as np
from jax import lax

D = 1024
HEADS = 16
HD = 64
FF = 2816
E = 16
V = 32128
BUCKETS = 32
TOPK = 2
STEPS = 4
REQ = 24
INNER = 1024
TOKENS = 96
CTX = 16384
CAP = 4


bucket_edges = np.array([int(math.ceil(16 * 8 ** (j / 16.0))) for j in range(1, 16)], np.int32)


def shared_lengths(key):
    sub_key = jax.random.fold_in(key, 7)
    key_one, key_two, key_three = jax.random.split(sub_key, 3)
    longest = CTX - STEPS
    first_draw = jax.random.randint(key_one, (REQ,), 0, longest + 1)
    second_draw = jax.random.randint(key_two, (REQ,), 0, longest + 1)
    lengths = 1 + first_draw * second_draw // (longest + 1)
    pick_row = jax.random.randint(key_three, (), 0, REQ)
    return jnp.where(jnp.arange(REQ) == pick_row, longest, lengths).astype(jnp.int32)


def draw_lengths(key, part):
    return shared_lengths(key)


def draw_buckets(key, part):
    lengths = shared_lengths(key)
    distance = lengths[:, None, None] + jnp.arange(STEPS, dtype=jnp.int32)[None, :, None] - jnp.arange(CTX, dtype=jnp.int32)[None, None, :]
    distance = jnp.maximum(distance, 0)
    far_bucket = 16 + jnp.sum((distance[..., None] >= jnp.asarray(bucket_edges)).astype(jnp.int32), axis=-1)
    return jnp.where(distance < 16, distance, far_bucket).astype(jnp.int32)


def draw_cache_keys(key, part):
    base = jnp.clip(jax.random.normal(jax.random.fold_in(key, 3), (REQ, CTX, INNER), jnp.float32), -6.0, 6.0)
    return base.astype(jnp.bfloat16)


def draw_rel_bias(key, part):
    key_one, key_two = jax.random.split(jax.random.fold_in(key, 9))
    slopes = jnp.exp(jax.random.uniform(key_one, (HEADS,), jnp.float32, math.log(0.02), math.log(0.8)))
    noise = 0.5 * jnp.clip(jax.random.normal(key_two, (BUCKETS, HEADS), jnp.float32), -3.0, 3.0)
    return -slopes[None, :] * jnp.arange(BUCKETS, dtype=jnp.float32)[:, None] + noise


def level_of(rng, dims, shards, low, largest):
    factor_of, own = 1.0, jax.random.fold_in(rng, 6)
    for axis_at, blocks in shards:
        steps = jnp.exp(jax.random.uniform(jax.random.fold_in(own, axis_at), (blocks,), jnp.float32, low / len(shards), largest / len(shards)))
        factor_of = factor_of * jnp.repeat(steps, dims[axis_at] // blocks).reshape([-1 if axis == axis_at else 1 for axis in range(len(dims))])
    return factor_of


def shared_out(own_key, own, number, rows, number_of, top, bound, skew):
    sequence = jax.random.permutation(own_key, number_of)
    packed, ordinary = portions_of(number_of, rows * top, bound, skew, True), portions_of(number_of, rows * top, bound, skew, False)
    places = jnp.arange(number_of)

    def named(tallies, turn):
        used = int((tallies > 0).sum())
        fixed = max(1, used // 4)
        shifted = fixed + (places - fixed + turn * (used - fixed)) % max(1, number_of - fixed)
        return jnp.zeros((number_of,), jnp.int32).at[sequence[jnp.where(places < fixed, places, shifted)]].set(jnp.asarray(tallies, jnp.int32))

    tallies = jnp.where(number % 4 == 0, named(packed, number // 4), named(ordinary, number - number // 4 - 1))
    mixed = jax.random.permutation(jax.random.fold_in(own, 3), number_of)
    giver, taker = mixed[0:number_of // 2 * 2:2], mixed[1:number_of // 2 * 2:2]
    room = jnp.minimum(tallies[giver] - 1, bound - tallies[taker]) // 2
    room = jnp.where((giver == sequence[0]) | (taker == sequence[0]) | (tallies[taker] == 0), 0, jnp.maximum(room, 0))
    shifted = jax.random.randint(jax.random.fold_in(own, 4), (number_of // 2,), 0, 1 << 20) % (room + 1)
    tallies = tallies.at[giver].add(-shifted).at[taker].add(shifted)
    items = jnp.searchsorted(jnp.cumsum(tallies), jnp.arange(rows * top), side="right").astype(jnp.int32)
    table = items.reshape(top, rows).T
    table = table[jax.random.permutation(jax.random.fold_in(own, 1), rows)]
    turn = jax.random.randint(jax.random.fold_in(own, 2), (rows, 1), 0, top)
    return jnp.take_along_axis(table, (jnp.arange(top)[None, :] + turn) % top, axis=1)


def portions_of(number_of, total, reach, slope, full):
    weights = [(1 << 20) // math.isqrt(grade ** slope) + 1 for grade in range(1, number_of + 1)]
    largest = reach if full else min(reach, max(-(-total // number_of), total * weights[0] // sum(weights)))
    least = 1 if total - largest >= number_of - 1 else 0
    holding, rest = [largest] + [least] * (number_of - 1), total - largest - least * (number_of - 1)
    while rest > 0:
        candidates = [i for i in range(1, number_of) if holding[i] < largest] or [i for i in range(1, number_of) if holding[i] < reach]
        whole, budget = sum([weights[i] for i in candidates]), rest
        for i in candidates:
            more = min(reach - holding[i], max(1, budget * weights[i] // whole), rest)
            holding[i] = holding[i] + more
            rest = rest - more
    return np.array(holding)


def scatter_about(key, shape, width, reach, shards=(), held_as=jnp.bfloat16):
    gain = level_of(key, shape, shards, -0.22, 0.18) if shards else 1.0
    values = jax.random.normal(key, shape, jnp.float32) * width * gain
    return jnp.minimum(jnp.maximum(values, -reach), reach).astype(held_as)


def setup_inputs(seed: int = 0) -> dict:
    streams_of = jax.random.split(jax.random.key(seed), 20)
    new_states = scatter_about(streams_of[0], (TOKENS, D), 1.0, 6.0)
    lengths = draw_lengths(jax.random.fold_in(streams_of[19], 71), 0)
    cache_keys = draw_cache_keys(jax.random.fold_in(streams_of[19], 71), 0)
    cache_values = scatter_about(streams_of[3], (REQ, CTX, INNER), 1.0, 6.0, ((1, 32), (2, 8)))
    buckets = draw_buckets(jax.random.fold_in(streams_of[19], 71), 0)
    attn_gain = jnp.clip(1.0 + 0.15 * jax.random.normal(streams_of[5], (D,), jnp.float32), 0.25, 1.75)
    w_query = scatter_about(streams_of[6], (D, INNER), (D * HD) ** -0.5, 0.0234375, ((1, 8),))
    w_key = scatter_about(streams_of[7], (D, INNER), D ** -0.5, 0.1875, ((1, 8),))
    w_value = scatter_about(streams_of[8], (D, INNER), D ** -0.5, 0.1875, ((1, 8),))
    rel_bias = draw_rel_bias(jax.random.fold_in(streams_of[19], 71), 0)
    w_out = scatter_about(streams_of[10], (INNER, D), INNER ** -0.5, 0.1875, ((0, 8),))
    ffn_gain = jnp.clip(1.0 + 0.15 * jax.random.normal(streams_of[11], (D,), jnp.float32), 0.25, 1.75)
    w_router = scatter_about(streams_of[12], (D, E), D ** -0.5, 0.1875, (), jnp.float32)
    w_gate = scatter_about(streams_of[13], (E, D, FF), D ** -0.5, 0.1875, ((0, 8), (2, 32)))
    w_up = scatter_about(streams_of[14], (E, D, FF), D ** -0.5, 0.1875, ((0, 8), (2, 32)))
    w_down = scatter_about(streams_of[15], (E, FF, D), FF ** -0.5, 0.109375, ((0, 8), (1, 32)))
    expert_picks_keys = jax.random.split(jax.random.fold_in(streams_of[16], 1), STEPS * REQ // REQ)
    expert_picks_turns = jax.random.permutation(jax.random.fold_in(streams_of[16], 3), STEPS * REQ // REQ)
    expert_picks = jax.vmap(lambda own, number: shared_out(jax.random.fold_in(streams_of[16], 2), own, number, REQ, E, TOPK, CAP, 2))(expert_picks_keys, expert_picks_turns).reshape((STEPS, REQ, TOPK))
    final_gain = jnp.clip(1.0 + 0.15 * jax.random.normal(streams_of[17], (D,), jnp.float32), 0.25, 1.75)
    w_vocab = scatter_about(streams_of[18], (D, V), (D // 9) ** -0.5, 0.5, ((1, 32),))
    return {"new_states": new_states, "lengths": lengths, "cache_keys": cache_keys, "cache_values": cache_values, "buckets": buckets, "attn_gain": attn_gain, "w_query": w_query, "w_key": w_key, "w_value": w_value, "rel_bias": rel_bias, "w_out": w_out, "ffn_gain": ffn_gain, "w_router": w_router, "w_gate": w_gate, "w_up": w_up, "w_down": w_down, "expert_picks": expert_picks, "final_gain": final_gain, "w_vocab": w_vocab}


def norm_parts(values, gain_row):
    norm_root = jnp.sqrt(lax.optimization_barrier(jnp.mean(values * values, axis=-1, keepdims=True)) + 1e-06)
    return (values / norm_root * gain_row, norm_root[..., 0])

def reference(new_states, lengths, cache_keys, cache_values, buckets, attn_gain, w_query, w_key, w_value, rel_bias, w_out, ffn_gain, w_router, w_gate, w_up, w_down, expert_picks, final_gain, w_vocab):
    states = new_states.astype(jnp.float32)
    scaled, _ = norm_parts(states, attn_gain)
    scaled = scaled.astype(jnp.bfloat16)
    queries = jnp.dot(scaled, w_query, preferred_element_type=jnp.float32).astype(jnp.bfloat16).reshape(REQ, STEPS, HEADS, HD)
    key_new = jnp.dot(scaled, w_key, preferred_element_type=jnp.float32).astype(jnp.bfloat16).reshape(REQ, STEPS, INNER)
    value_new = jnp.dot(scaled, w_value, preferred_element_type=jnp.float32).astype(jnp.bfloat16).reshape(REQ, STEPS, INNER)

    def attend(operands):
        query_rows, key_fresh, value_fresh, key_cache, value_cache, bucket_rows, length = operands
        key_rows = lax.dynamic_update_slice(key_cache, key_fresh, (length, jnp.int32(0)))
        value_rows = lax.dynamic_update_slice(value_cache, value_fresh, (length, jnp.int32(0)))
        key_heads = key_rows.astype(jnp.float32).reshape(CTX, HEADS, HD)
        value_heads = value_rows.astype(jnp.float32).reshape(CTX, HEADS, HD)
        scores = jnp.einsum('thd,phd->thp', query_rows.astype(jnp.float32), key_heads, precision=lax.Precision.HIGHEST)
        bias_rows = rel_bias[bucket_rows]
        scores = scores + jnp.transpose(bias_rows, (0, 2, 1))
        position = jnp.arange(CTX, dtype=jnp.int32)
        allowed = position[None, :] <= length + jnp.arange(STEPS, dtype=jnp.int32)[:, None]
        scores = jnp.where(allowed[:, None, :], scores, -1e+30)
        row_top = lax.optimization_barrier(jnp.max(scores, axis=-1, keepdims=True))
        weights = jnp.where(allowed[:, None, :], jnp.exp(scores - row_top), 0.0)
        numerator = jnp.einsum('thp,phd->thd', weights, value_heads, precision=lax.Precision.HIGHEST)
        return numerator / lax.optimization_barrier(jnp.sum(weights, axis=-1))[..., None]
    heads_out = lax.map(attend, (queries, key_new, value_new, cache_keys, cache_values, buckets, lengths))
    mixed_rows = jnp.dot(heads_out.reshape(TOKENS, INNER), w_out.astype(jnp.float32), precision=lax.Precision.HIGHEST)
    hidden_one = states + mixed_rows
    normed, _ = norm_parts(hidden_one, ffn_gain)
    router_logits = jnp.dot(normed, w_router, precision=lax.Precision.HIGHEST)
    normed_low = normed.astype(jnp.bfloat16)
    expert_ids = jnp.arange(E, dtype=jnp.int32)
    pick_marks = (expert_picks[..., None] == expert_ids).astype(jnp.int32)
    per_step = lax.optimization_barrier(jnp.sum(pick_marks, axis=2))
    earlier = jnp.cumsum(per_step, axis=1) - per_step
    slot_index = lax.optimization_barrier(jnp.sum(pick_marks * earlier[:, :, None, :], axis=-1))
    token_picks = jnp.transpose(expert_picks, (1, 0, 2)).reshape(TOKENS, TOPK)
    token_slots = jnp.transpose(slot_index, (1, 0, 2)).reshape(TOKENS, TOPK)
    token_steps = jnp.arange(TOKENS, dtype=jnp.int32) % STEPS
    row_index = token_picks * (STEPS * CAP) + token_steps[:, None] * CAP + token_slots
    picked = jnp.take_along_axis(router_logits, token_picks, axis=1)
    gate_first = jax.nn.sigmoid(picked[:, 0] - picked[:, 1])
    gate_second = jax.nn.sigmoid(picked[:, 1] - picked[:, 0])
    dispatched = jnp.zeros((E * STEPS * CAP, D), jnp.bfloat16)
    dispatched = dispatched.at[row_index[:, 0]].set(normed_low).at[row_index[:, 1]].set(normed_low)

    def expert(operands):
        routed, gate_weight, up_weight, down_weight = operands
        gate_values = jnp.dot(routed, gate_weight, preferred_element_type=jnp.float32)
        up_values = jnp.dot(routed, up_weight, preferred_element_type=jnp.float32)
        hidden = (jax.nn.gelu(gate_values, approximate=True) * up_values).astype(jnp.bfloat16)
        return jnp.dot(hidden, down_weight, preferred_element_type=jnp.float32).astype(jnp.bfloat16)
    expert_out = lax.map(expert, (dispatched.reshape(E, STEPS * CAP, D), w_gate, w_up, w_down)).reshape(E * STEPS * CAP, D)
    expert_mix = gate_first[:, None] * expert_out[row_index[:, 0]].astype(jnp.float32) + gate_second[:, None] * expert_out[row_index[:, 1]].astype(jnp.float32)
    final_rows = (hidden_one + expert_mix).astype(jnp.bfloat16)
    scaled_out, norm_root = norm_parts(final_rows.astype(jnp.float32), final_gain)
    logits = jnp.dot(scaled_out.astype(jnp.bfloat16), w_vocab, preferred_element_type=jnp.float32)
    return (final_rows, norm_root, lax.optimization_barrier(jnp.max(logits, axis=-1)))
```

```python
import functools

import jax
import jax.numpy as jnp
from jax import lax
from jax.experimental import pallas as pl
from jax.experimental.pallas import tpu as pltpu
from jax.sharding import PartitionSpec as P

F32 = jnp.float32
BF16 = jnp.bfloat16
CAP = 4
EPS = 1e-06
LOW = -1e30
MESH = pl.DeviceIdType.MESH
NT = (((1,), (1,)), ((), ()))
HIGH = lax.Precision.HIGHEST


def iota(shape, dim):
    return lax.broadcasted_iota(jnp.int32, shape, dim)


def dot(a, b):
    return jnp.dot(a, b, preferred_element_type=F32)


def dot_nt(a, b, precision=None):
    return lax.dot_general(a, b, NT, precision=precision, preferred_element_type=F32)


def local_kernel(
    per,
    len_ref,
    x_ref,
    ag_ref,
    wq_ref,
    wk_ref,
    wv_ref,
    rb_ref,
    pk_ref,
    k_ref,
    v_ref,
    b_ref,
    a_ref,
    chl_ref,
    chr_ref,
    cbl_ref,
    cbr_ref,
    eo_ref,
    q_sc,
    kn_sc,
    vn_sc,
    tb_sc,
):
    step = pl.program_id(0)
    seq = lax.axis_index("seq")
    head = lax.axis_index("head")
    row = iota((8, 128), 0)
    lane = iota((8, 128), 1)
    own = (lane < 64) == (row < 4)

    @pl.when(step == 0)
    def _():
        x = x_ref[...].astype(F32)
        root = jnp.sqrt(jnp.mean(x * x, axis=-1, keepdims=True) + EPS)
        scaled = (x / root * ag_ref[...]).astype(BF16)
        i, j = iota((192, 96), 0), iota((192, 96), 1)
        spread = jnp.where(j == (i // 8) * 4 + i % 4, 1.0, 0.0).astype(BF16)
        keep = (iota((192, 128), 1) < 64) == (iota((192, 128), 0) % 8 < 4)
        q = dot(spread, dot(scaled, wq_ref[...]).astype(BF16))
        q_sc[...] = jnp.where(keep, q, 0.0).reshape(24, 8, 128)
        kn_sc[...] = dot(spread, dot(scaled, wk_ref[...]).astype(BF16)).reshape(24, 8, 128)
        v = dot(spread, dot(scaled, wv_ref[...]).astype(BF16))
        v = jnp.where(iota((192, 128), 0) % 8 < 4, v, 0.0)
        vn_sc[...] = v.reshape(24, 8, 128)
        tb_sc[...] = jnp.zeros((8, 128), F32)
        tb_sc[:, 0:32] = jnp.where(iota((8, 32), 0) < 4, rb_ref[0:1, :], rb_ref[1:2, :])
        i = iota((32, 24), 0)
        e, t, c = head * 2 + i // 16, (i // 4) % 4, i % 4
        p0 = jnp.zeros((32, 24), jnp.int32)
        p1 = jnp.zeros((32, 24), jnp.int32)
        for s in range(4):
            p0 = jnp.where(t == s, pk_ref[s : s + 1, :], p0)
            p1 = jnp.where(t == s, pk_ref[4 + s : 5 + s, :], p1)
        inc = jnp.where((p0 == e) | (p1 == e), 1.0, 0.0)
        upper = jnp.where(iota((24, 24), 0) < iota((24, 24), 1), 1.0, 0.0)
        before = dot(inc.astype(BF16), upper.astype(BF16))
        ch = jnp.where(before == c.astype(F32), inc, 0.0)
        other = jnp.sum(ch * (p0 + p1 - e).astype(F32), axis=1, keepdims=True)
        n = iota((32, 16), 1)
        e16 = head * 2 + iota((32, 16), 0) // 16
        eo_ref[...] = jnp.where(n == e16, 1.0, 0.0) - jnp.where(n.astype(F32) == other, 1.0, 0.0)
        ch = ch.astype(BF16)
        grow = jnp.where(iota((24, 192), 1) // 8 == iota((24, 192), 0), 1.0, 0.0).astype(BF16)
        wide = dot(ch, grow)
        l8, t_r = iota((32, 192), 1) % 8, (iota((32, 192), 0) // 4) % 4
        chl_ref[...] = jnp.where(l8 == t_r, wide, 0.0).astype(BF16)
        chr_ref[...] = jnp.where(l8 == t_r + 4, wide, 0.0).astype(BF16)
        grow_t = jnp.where(iota((192, 24), 0) // 8 == iota((192, 24), 1), 1.0, 0.0).astype(BF16)
        tall = dot_nt(grow_t, ch)
        r8, t_l = iota((192, 32), 0) % 8, (iota((192, 32), 1) // 4) % 4
        cbl_ref[...] = jnp.where(r8 == t_l, tall, 0.0).astype(BF16)
        cbr_ref[...] = jnp.where(r8 == t_l + 4, tall, 0.0).astype(BF16)

    span = k_ref.shape[1]
    wide_row = iota((8, span), 0)
    wide_pos = iota((8, span), 1) + seq * span
    table = tb_sc[...]
    for i in range(per):
        r = step * per + i
        rel = wide_pos - len_ref[r]
        q8 = q_sc[r].astype(BF16)
        scores = dot_nt(q8, k_ref[i])
        fresh = dot_nt(q8, kn_sc[r].astype(BF16))
        for t in range(4):
            scores = jnp.where(rel == t, fresh[:, t : t + 1], scores)
        b4 = b_ref[i]
        b8 = jnp.concatenate([b4, b4], axis=0)
        bias = jnp.concatenate(
            [
                jnp.take_along_axis(
                    table, b8[:, c * 128 : c * 128 + 128], axis=1, mode="promise_in_bounds"
                )
                for c in range(span // 128)
            ],
            axis=1,
        )
        allowed = rel <= wide_row % 4
        scores = jnp.where(allowed, scores + bias, LOW)
        top = jnp.max(scores, axis=1, keepdims=True)
        weights = jnp.where(allowed, jnp.exp(scores - top), 0.0)
        mass = jnp.sum(weights, axis=1, keepdims=True)
        landed = (rel >= 0) & (rel < 4)
        hot = jnp.where(rel == wide_row, 1.0, 0.0).astype(BF16)
        summed = dot(jnp.where(landed, 0.0, weights).astype(BF16), v_ref[i])
        w_new = dot_nt(weights.astype(BF16), hot)
        summed = summed + dot(w_new.astype(BF16), vn_sc[r].astype(BF16))
        a_ref[i] = jnp.where(own, summed, jnp.where(lane % 64 < 32, top, mass))


def exchange_kernel(
    a_ref,
    x_ref,
    wo_ref,
    fg_ref,
    wr_ref,
    chl_ref,
    chr_ref,
    cbl_ref,
    cbr_ref,
    eo_ref,
    og_ref,
    wg_hbm,
    wu_hbm,
    wd_hbm,
    wv_hbm,
    fin_ref,
    stat_ref,
    wg,
    wu,
    wd,
    wv,
    in1,
    out2,
    in2,
    out3,
    in3,
    out4,
    in4,
    out5,
    in5,
    out6,
    in6,
    out7,
    in7,
    hid,
    load_sem,
    send_sem,
    recv_sem,
    fin_sem,
):
    seq_count, head_count = 32, 8
    me = lax.axis_index("seq")
    z = lax.axis_index("head")
    owner = me % 4 != 3
    mine = (me // 4) * 3 + me % 4
    home = me // 4

    loads = [
        pltpu.make_async_copy(src, dst, load_sem.at[n])
        for n, (src, dst) in enumerate(((wg_hbm, wg), (wu_hbm, wu), (wd_hbm, wd), (wv_hbm, wv)))
    ]
    for load in loads:
        load.start()

    barrier = pltpu.get_barrier_semaphore()

    @pl.loop(1, seq_count)
    def _(n):
        pl.semaphore_signal(
            barrier, inc=1, device_id={"seq": (me + n) % seq_count}, device_id_type=MESH
        )

    @pl.loop(1, head_count)
    def _(n):
        pl.semaphore_signal(
            barrier, inc=1, device_id={"head": (z + n) % head_count}, device_id_type=MESH
        )

    pl.semaphore_wait(barrier, seq_count + head_count - 2)

    def send(stage, src, dst, target, sem=None):
        pltpu.make_async_remote_copy(
            src_ref=src,
            dst_ref=dst,
            send_sem=send_sem.at[stage],
            recv_sem=recv_sem.at[stage] if sem is None else sem,
            device_id=target,
            device_id_type=MESH,
        ).start()

    def await_bytes(ref, sem):
        pltpu.make_async_copy(ref, ref, sem).wait()

    row = iota((8, 512), 0)
    upper = row < 4

    def fold(rows):
        return jnp.where(upper, rows[:, :512], rows[:, 512:])

    def pair_mean(values):
        total = jnp.sum(values * values, axis=1, keepdims=True)
        return (total + jnp.concatenate([total[4:8], total[0:4]], axis=0)) / 1024.0

    @pl.loop(1, seq_count)
    def _(n):
        target = (me + n) % seq_count

        @pl.when(target % 4 != 3)
        def _():
            request = (target // 4) * 3 + target % 4
            send(0, a_ref.at[request], in1.at[n], {"seq": target})

    @pl.when(owner)
    def _():
        in1[0] = a_ref[mine]
        i, j = iota((8, 96), 0), iota((8, 96), 1)
        pick = jnp.where(j == mine * 4 + i % 4, 1.0, 0.0).astype(BF16)
        states = fold(dot(pick, x_ref[...]))
        await_bytes(in1.at[pl.ds(0, 31)], recv_sem.at[0])
        part = in1[...]
        r3, l3 = iota((32, 8, 128), 1), iota((32, 8, 128), 2)
        spare = (l3 < 64) != (r3 < 4)
        tops = jnp.max(
            jnp.where(spare & (l3 % 64 < 32), part, -3e38), axis=2, keepdims=True
        )
        masses = jnp.max(
            jnp.where(spare & (l3 % 64 >= 32), part, -3e38), axis=2, keepdims=True
        )
        lead = jnp.exp(tops - jnp.max(tops, axis=0, keepdims=True))
        mass = jnp.sum(masses * lead, axis=0)
        both = jnp.sum(part * lead, axis=0) / mass
        swapped = jnp.concatenate([both[4:8], both[0:4]], axis=0)
        mixed = jnp.where((iota((8, 128), 1) < 64) == (iota((8, 128), 0) < 4), both, swapped)
        coarse = mixed.astype(BF16)
        fine = (mixed - coarse.astype(F32)).astype(BF16)
        wo = wo_ref[...]
        term = fold(dot(coarse, wo) + dot(fine, wo)).astype(BF16)
        out2[...] = term
        in2[z] = term

        @pl.loop(1, head_count)
        def _(n):
            send(1, out2, in2.at[z], {"head": (z + n) % head_count})

        await_bytes(in2.at[pl.ds(0, 7)], recv_sem.at[1])
        hidden = states + jnp.sum(in2[...].astype(F32), axis=0)
        hid[...] = hidden
        gain = jnp.where(upper, fg_ref[:, :512], fg_ref[:, 512:])
        normed = (hidden / jnp.sqrt(pair_mean(hidden) + EPS) * gain).astype(BF16)
        out3[...] = normed
        in3[mine] = normed

        @pl.loop(1, seq_count)
        def _(n):
            send(2, out3, in3.at[mine], {"seq": (me + n) % seq_count})

        await_bytes(in3.at[pl.ds(0, 23)], recv_sem.at[2])

    @pl.when(me % 4 == 3)
    def _():
        await_bytes(in3, recv_sem.at[2])

    rows = in3[...].astype(F32).reshape(192, 512).astype(BF16)
    routed = jnp.concatenate([dot(chl_ref[...], rows), dot(chr_ref[...], rows)], axis=1)
    logits = dot_nt(routed, wr_ref[...], HIGH)
    delta = jnp.sum(logits * eo_ref[...], axis=1, keepdims=True)
    gate = 1.0 / (1.0 + jnp.exp(-delta))
    routed = routed.astype(BF16)
    for load in loads[:3]:
        load.wait()
    downs = []
    for e in range(2):
        slots = routed[e * 16 : e * 16 + 16]
        gated = jax.nn.gelu(dot_nt(slots, wg[e]), approximate=True)
        units = (gated * dot_nt(slots, wu[e])).astype(BF16)
        downs.append(dot(units, wd[e]))
    down = (jnp.concatenate(downs, axis=0) * gate).astype(BF16)
    spread = dot(cbl_ref[...], down[:, :512]) + dot(cbr_ref[...], down[:, 512:])
    out4[...] = spread.reshape(24, 8, 512).astype(BF16)

    @pl.loop(1, seq_count)
    def _(n):
        target = (me + n) % seq_count

        @pl.when(target % 4 != 3)
        def _():
            request = (target // 4) * 3 + target % 4
            send(3, out4.at[request], in4.at[n], {"seq": target})

    @pl.when(owner)
    def _():
        in4[0] = out4[mine]
        await_bytes(in4.at[pl.ds(0, 31)], recv_sem.at[3])
        mix = jnp.sum(in4[...].astype(F32), axis=0)

        @pl.when(z != home)
        def _():
            out5[...] = mix.astype(BF16)
            send(4, out5, in5.at[z], {"head": home})

        @pl.when(z == home)
        def _():
            in5[z] = mix.astype(BF16)
            await_bytes(in5.at[pl.ds(0, 7)], recv_sem.at[4])
            final = (hid[...] + jnp.sum(in5[...].astype(F32), axis=0)).astype(BF16)
            out6[...] = final
            in6[me % 4] = final

            @pl.loop(1, seq_count)
            def _(n):
                send(
                    5,
                    out6,
                    in6.at[me % 4],
                    {"seq": (me + n) % seq_count},
                    fin_sem.at[me % 4],
                )

    for k in range(3):

        @pl.when(me != z * 4 + k)
        def _():
            await_bytes(in6.at[k], fin_sem.at[k])

    rows = in6[...].astype(F32)
    total = jnp.sum(rows * rows, axis=2, keepdims=True)
    total = total + jnp.concatenate([total[:, 4:8], total[:, 0:4]], axis=1)
    root = jnp.sqrt(total / 1024.0 + EPS)
    gain = jnp.where(upper, og_ref[:, :512], og_ref[:, 512:])
    scaled = (rows / root * gain[None]).reshape(24, 512).astype(BF16)
    loads[3].wait()
    left = dot_nt(scaled, wv[:, :512])
    right = dot_nt(scaled, wv[:, 512:])
    width = wv.shape[0]
    left = left.reshape(3, 8, width)[:, 0:4]
    right = right.reshape(3, 8, width)[:, 4:8]
    best = jnp.max(left + right, axis=2, keepdims=True)
    token = iota((3, 4, 128), 0) * 4 + iota((3, 4, 128), 1)
    place = iota((3, 4, 128), 2) == token
    best = jnp.sum(jnp.sum(jnp.where(place, best, 0.0), axis=0), axis=0, keepdims=True)
    roots = jnp.sum(jnp.sum(jnp.where(place, root[:, 0:4], 0.0), axis=0), axis=0, keepdims=True)
    best = jnp.broadcast_to(best, (8, 128))
    out7[...] = best
    in7[0] = best

    @pl.loop(1, seq_count)
    def _(n):
        send(6, out7, in7.at[n], {"seq": (me + n) % seq_count})

    halves = [jnp.concatenate([rows[k, 0:4], rows[k, 4:8]], axis=1) for k in range(3)]
    fin_ref[...] = jnp.concatenate(halves, axis=0).astype(BF16)
    await_bytes(in7.at[pl.ds(0, 31)], recv_sem.at[6])
    best = jnp.max(in7[...], axis=0)
    stat_ref[...] = jnp.where(iota((8, 128), 0) == 0, roots, best)

    @pl.when(owner)
    def _():
        await_bytes(a_ref.at[pl.ds(0, 23)], send_sem.at[0])
        await_bytes(in2.at[pl.ds(0, 7)], send_sem.at[1])
        await_bytes(in4.at[pl.ds(0, 31)], send_sem.at[2])
        await_bytes(out4.at[pl.ds(0, 23)], send_sem.at[3])

        @pl.when(z != home)
        def _():
            await_bytes(out5, send_sem.at[4])

        @pl.when(z == home)
        def _():
            await_bytes(in4.at[pl.ds(0, 31)], send_sem.at[5])

    @pl.when(me % 4 == 3)
    def _():
        await_bytes(a_ref, send_sem.at[0])
        await_bytes(out4, send_sem.at[3])

    await_bytes(in7.at[pl.ds(0, 31)], send_sem.at[6])


def shards(
    new_states,
    lengths,
    cache_keys,
    cache_values,
    buckets,
    attn_gain,
    w_query,
    w_key,
    w_value,
    rel_bias,
    w_out,
    ffn_gain,
    w_router,
    w_gate,
    w_up,
    w_down,
    expert_picks,
    final_gain,
    w_vocab,
):
    requests, span, inner = cache_keys.shape
    per = 6
    whole = pl.BlockSpec(memory_space=pltpu.VMEM)
    smem = pl.BlockSpec(memory_space=pltpu.SMEM)
    anywhere = pl.BlockSpec(memory_space=pl.ANY)
    picks = jnp.transpose(expert_picks, (2, 0, 1)).reshape(8, requests)

    def fixed(shape):
        return pl.BlockSpec(shape, lambda i: (0,) * len(shape))

    shapes = [(32, 192), (32, 192), (192, 32), (192, 32), (32, 16)]
    types = [BF16, BF16, BF16, BF16, F32]
    tables = pl.pallas_call(
        functools.partial(local_kernel, per),
        grid=(requests // per,),
        out_shape=[jax.ShapeDtypeStruct((requests, 8, 128), F32)]
        + [jax.ShapeDtypeStruct(s, t) for s, t in zip(shapes, types)],
        in_specs=[smem]
        + [fixed(s) for s in ((96, 1024), (1, 1024), (1024, 128), (1024, 128), (1024, 128), (2, 32), (8, 24))]
        + [
            pl.BlockSpec((per, span, inner), lambda i: (i, 0, 0)),
            pl.BlockSpec((per, span, inner), lambda i: (i, 0, 0)),
            pl.BlockSpec((per, 4, span), lambda i: (i, 0, 0)),
        ],
        out_specs=[pl.BlockSpec((per, 8, 128), lambda i: (i, 0, 0))] + [fixed(s) for s in shapes],
        scratch_shapes=[pltpu.VMEM((24, 8, 128), F32)] * 3 + [pltpu.VMEM((8, 128), F32)],
        name="local_attention",
    )(
        lengths,
        new_states,
        attn_gain[None],
        w_query,
        w_key,
        w_value,
        rel_bias.T,
        picks,
        cache_keys,
        cache_values,
        buckets,
    )
    partial, rest = tables[0], tables[1:]
    vocab = w_vocab.T
    final, stats = pl.pallas_call(
        exchange_kernel,
        out_shape=(
            jax.ShapeDtypeStruct((12, 1024), BF16),
            jax.ShapeDtypeStruct((8, 128), F32),
        ),
        in_specs=[whole] * 11 + [anywhere] * 4,
        out_specs=(whole, whole),
        scratch_shapes=[
            pltpu.VMEM((2, 88, 1024), BF16),
            pltpu.VMEM((2, 88, 1024), BF16),
            pltpu.VMEM((2, 88, 1024), BF16),
            pltpu.VMEM(vocab.shape, BF16),
            pltpu.VMEM((32, 8, 128), F32),
            pltpu.VMEM((8, 512), BF16),
            pltpu.VMEM((8, 8, 512), BF16),
            pltpu.VMEM((8, 512), BF16),
            pltpu.VMEM((24, 8, 512), BF16),
            pltpu.VMEM((24, 8, 512), BF16),
            pltpu.VMEM((32, 8, 512), BF16),
            pltpu.VMEM((8, 512), BF16),
            pltpu.VMEM((8, 8, 512), BF16),
            pltpu.VMEM((8, 512), BF16),
            pltpu.VMEM((3, 8, 512), BF16),
            pltpu.VMEM((8, 128), F32),
            pltpu.VMEM((32, 8, 128), F32),
            pltpu.VMEM((8, 512), F32),
            pltpu.SemaphoreType.DMA((4,)),
            pltpu.SemaphoreType.DMA((7,)),
            pltpu.SemaphoreType.DMA((7,)),
            pltpu.SemaphoreType.DMA((3,)),
        ],
        compiler_params=pltpu.CompilerParams(collective_id=0, has_side_effects=True),
        name="exchange",
    )(
        partial,
        new_states,
        w_out,
        ffn_gain[None],
        w_router.T,
        *rest,
        final_gain[None],
        jnp.transpose(w_gate, (0, 2, 1)),
        jnp.transpose(w_up, (0, 2, 1)),
        w_down,
        vocab,
    )
    return final, stats[0, :12], stats[1, :12]


def solution(mesh):
    placed = (
        P(),
        P(),
        P(None, "seq", "head"),
        P(None, "seq", "head"),
        P(None, None, "seq"),
        P(),
        P(None, "head"),
        P(None, "head"),
        P(None, "head"),
        P(None, "head"),
        P("head", None),
        P(),
        P(),
        P("head", None, "seq"),
        P("head", None, "seq"),
        P("head", "seq", None),
        P(),
        P(),
        P(None, "seq"),
    )
    return jax.shard_map(
        shards,
        mesh=mesh,
        in_specs=placed,
        out_specs=(P("head", None), P("head"), P("head")),
        check_vma=False,
    )
```

```python
import functools

import jax
import jax.numpy as jnp
from jax import lax
from jax.experimental import pallas as pl
from jax.experimental.pallas import tpu as pltpu
from jax.sharding import PartitionSpec as P

F32 = jnp.float32
BF16 = jnp.bfloat16
CAP = 4
EPS = 1e-06
LOW = -1e30
MESH = pl.DeviceIdType.MESH
NT = (((1,), (1,)), ((), ()))
HIGH = lax.Precision.HIGHEST


def iota(shape, dim):
    return lax.broadcasted_iota(jnp.int32, shape, dim)


def dot(a, b):
    return jnp.dot(a, b, preferred_element_type=F32)


def dot_nt(a, b, precision=None):
    return lax.dot_general(a, b, NT, precision=precision, preferred_element_type=F32)


def layer_kernel(
    per,
    len_ref,
    ag_ref,
    rb_ref,
    pk_ref,
    fg_ref,
    wr_ref,
    og_ref,
    x_hbm,
    wq_hbm,
    wk_hbm,
    wv_hbm,
    k_hbm,
    v_hbm,
    b_hbm,
    wo_hbm,
    wg_hbm,
    wu_hbm,
    wd_hbm,
    voc_hbm,
    fin_ref,
    stat_ref,
    xb,
    wq,
    wk,
    wv,
    kb,
    vb,
    bb,
    wo,
    wg,
    wu,
    wd,
    voc,
    q_sc,
    kn_sc,
    vn_sc,
    tb_sc,
    chl_sc,
    chr_sc,
    cbl_sc,
    cbr_sc,
    eo_sc,
    wr_sc,
    part_sc,
    in1,
    out2,
    in2,
    out3,
    in3,
    out4,
    in4,
    out5,
    in5,
    out6,
    in6,
    out7,
    in7,
    hid,
    load_sem,
    k_sem,
    v_sem,
    send_sem,
    recv_sem,
    fin_sem,
):
    seq_count, head_count = 32, 8
    me = lax.axis_index("seq")
    z = lax.axis_index("head")
    owner = me % 4 != 3
    mine = (me // 4) * 3 + me % 4
    home = me // 4
    requests, span = kb.shape[0], kb.shape[1]
    chunks = requests // per

    def cache_load(src, dst, sem, c):
        rows = pl.ds(c * per, per)
        return pltpu.make_async_copy(src.at[rows], dst.at[rows], sem.at[c])

    first = [(x_hbm, xb), (wq_hbm, wq), (wk_hbm, wk), (wv_hbm, wv), (b_hbm, bb)]
    later = [(wo_hbm, wo), (wg_hbm, wg), (wu_hbm, wu), (wd_hbm, wd), (voc_hbm, voc)]
    loads = [
        pltpu.make_async_copy(src, dst, load_sem.at[n]) for n, (src, dst) in enumerate(first + later)
    ]
    for load in loads[:5]:
        load.start()
    for c in range(chunks):
        cache_load(k_hbm, kb, k_sem, c).start()
        cache_load(v_hbm, vb, v_sem, c).start()
    for load in loads[5:]:
        load.start()

    barrier = pltpu.get_barrier_semaphore()

    @pl.loop(1, seq_count)
    def _(n):
        pl.semaphore_signal(
            barrier, inc=1, device_id={"seq": (me + n) % seq_count}, device_id_type=MESH
        )

    @pl.loop(1, head_count)
    def _(n):
        pl.semaphore_signal(
            barrier, inc=1, device_id={"head": (z + n) % head_count}, device_id_type=MESH
        )

    def send(stage, src, dst, target, sem=None):
        pltpu.make_async_remote_copy(
            src_ref=src,
            dst_ref=dst,
            send_sem=send_sem.at[stage],
            recv_sem=recv_sem.at[stage] if sem is None else sem,
            device_id=target,
            device_id_type=MESH,
        ).start()

    def await_bytes(ref, sem):
        pltpu.make_async_copy(ref, ref, sem).wait()

    i = iota((32, 24), 0)
    e, t, c = z * 2 + i // 16, (i // 4) % 4, i % 4
    p0 = jnp.zeros((32, 24), jnp.int32)
    p1 = jnp.zeros((32, 24), jnp.int32)
    for s in range(4):
        p0 = jnp.where(t == s, pk_ref[s, 0:1, :], p0)
        p1 = jnp.where(t == s, pk_ref[s, 1:2, :], p1)
    inc = jnp.where((p0 == e) | (p1 == e), 1.0, 0.0)
    before = jnp.where(iota((24, 24), 0) < iota((24, 24), 1), 1.0, 0.0)
    before = dot(inc.astype(BF16), before.astype(BF16))
    ch = jnp.where(before == c.astype(F32), inc, 0.0)
    other = jnp.sum(ch * (p0 + p1 - e).astype(F32), axis=1, keepdims=True)
    n = iota((32, 32), 1) % 16
    e16 = z * 2 + iota((32, 32), 0) // 16
    eo_sc[...] = jnp.where(n == e16, 1.0, 0.0) - jnp.where(n.astype(F32) == other, 1.0, 0.0)
    ch = ch.astype(BF16)
    grow = jnp.where(iota((24, 192), 1) // 8 == iota((24, 192), 0), 1.0, 0.0).astype(BF16)
    wide = dot(ch, grow)
    l8, t_r = iota((32, 192), 1) % 8, (iota((32, 192), 0) // 4) % 4
    chl_sc[...] = jnp.where(l8 == t_r, wide, 0.0).astype(BF16)
    chr_sc[...] = jnp.where(l8 == t_r + 4, wide, 0.0).astype(BF16)
    grow_t = jnp.where(iota((192, 24), 0) // 8 == iota((192, 24), 1), 1.0, 0.0).astype(BF16)
    tall = dot_nt(grow_t, ch)
    r8, t_l = iota((192, 32), 0) % 8, (iota((192, 32), 1) // 4) % 4
    cbl_sc[...] = jnp.where(r8 == t_l, tall, 0.0).astype(BF16)
    cbr_sc[...] = jnp.where(r8 == t_l + 4, tall, 0.0).astype(BF16)
    router = wr_ref[...]
    coarse = router.astype(BF16)
    wr_sc[0:16] = coarse
    wr_sc[16:32] = (router - coarse.astype(F32)).astype(BF16)
    tb_sc[...] = jnp.zeros((8, 128), F32)
    tb_sc[:, 0:32] = jnp.where(iota((8, 32), 0) < 4, rb_ref[0:1, :], rb_ref[1:2, :])

    for load in loads[:4]:
        load.wait()
    x = xb[...].astype(F32)
    root = jnp.sqrt(jnp.mean(x * x, axis=-1, keepdims=True) + EPS)
    scaled = (x / root * ag_ref[...]).astype(BF16)
    i, j = iota((192, 96), 0), iota((192, 96), 1)
    spread = jnp.where(j == (i // 8) * 4 + i % 4, 1.0, 0.0).astype(BF16)
    front = iota((192, 128), 0) % 8 < 4
    q = dot(spread, dot(scaled, wq[...]).astype(BF16))
    q = jnp.where((iota((192, 128), 1) < 64) == front, q, 0.0)
    q_sc[...] = q.reshape(24, 8, 128)
    kn_sc[...] = dot(spread, dot(scaled, wk[...]).astype(BF16)).reshape(24, 8, 128)
    v = dot(spread, dot(scaled, wv[...]).astype(BF16))
    vn_sc[...] = jnp.where(front, v, 0.0).reshape(24, 8, 128)

    loads[4].wait()
    pl.semaphore_wait(barrier, seq_count + head_count - 2)

    row8, lane8 = iota((8, 128), 0), iota((8, 128), 1)
    own = (lane8 < 64) == (row8 < 4)
    wide_row = iota((8, span), 0)
    wide_pos = iota((8, span), 1) + me * span
    table = tb_sc[...]

    def attend(r):
        rel = wide_pos - len_ref[r]
        q8 = q_sc[r].astype(BF16)
        scores = dot_nt(q8, kb[r])
        fresh = dot_nt(q8, kn_sc[r].astype(BF16))
        for t in range(4):
            scores = jnp.where(rel == t, fresh[:, t : t + 1], scores)
        b4 = bb[r]
        b8 = jnp.concatenate([b4, b4], axis=0)
        bias = jnp.concatenate(
            [
                jnp.take_along_axis(
                    table, b8[:, c * 128 : c * 128 + 128], axis=1, mode="promise_in_bounds"
                )
                for c in range(span // 128)
            ],
            axis=1,
        )
        allowed = rel <= wide_row % 4
        scores = jnp.where(allowed, scores + bias, LOW)
        top = jnp.max(scores, axis=1, keepdims=True)
        weights = jnp.where(allowed, jnp.exp(scores - top), 0.0)
        mass = jnp.sum(weights, axis=1, keepdims=True)
        landed = (rel >= 0) & (rel < 4)
        hot = jnp.where(rel == wide_row, 1.0, 0.0).astype(BF16)
        summed = dot(jnp.where(landed, 0.0, weights).astype(BF16), vb[r])
        w_new = dot_nt(weights.astype(BF16), hot)
        summed = summed + dot(w_new.astype(BF16), vn_sc[r].astype(BF16))
        return jnp.where(own, summed, jnp.where(lane8 % 64 < 32, top, mass))

    @pl.loop(0, chunks)
    def _(c):
        cache_load(k_hbm, kb, k_sem, c).wait()
        cache_load(v_hbm, vb, v_sem, c).wait()
        tiles = [attend(c * per + i) for i in range(per)]
        for i in range(per):
            part_sc[c * per + i] = tiles[i]
        for i in range(per):
            r = c * per + i
            target = r + r // 3

            @pl.when(target != me)
            def _():
                slot = (target - me + seq_count) % seq_count
                send(0, part_sc.at[r], in1.at[slot], {"seq": target})

    upper = iota((8, 512), 0) < 4

    def fold(rows):
        return jnp.where(upper, rows[:, :512], rows[:, 512:])

    def pair_mean(values):
        total = jnp.sum(values * values, axis=1, keepdims=True)
        return (total + jnp.concatenate([total[4:8], total[0:4]], axis=0)) / 1024.0

    loads[5].wait()

    @pl.when(owner)
    def _():
        in1[0] = part_sc[mine]
        i, j = iota((8, 96), 0), iota((8, 96), 1)
        pick = jnp.where(j == mine * 4 + i % 4, 1.0, 0.0).astype(BF16)
        states = fold(dot(pick, xb[...]))
        await_bytes(in1.at[pl.ds(0, 31)], recv_sem.at[0])
        part = in1[...]
        r3, l3 = iota((32, 8, 128), 1), iota((32, 8, 128), 2)
        spare = (l3 < 64) != (r3 < 4)
        tops = jnp.max(jnp.where(spare & (l3 % 64 < 32), part, -3e38), axis=2, keepdims=True)
        masses = jnp.max(jnp.where(spare & (l3 % 64 >= 32), part, -3e38), axis=2, keepdims=True)
        lead = jnp.exp(tops - jnp.max(tops, axis=0, keepdims=True))
        mass = jnp.sum(masses * lead, axis=0)
        both = jnp.sum(part * lead, axis=0) / mass
        swapped = jnp.concatenate([both[4:8], both[0:4]], axis=0)
        mixed = jnp.where(own, both, swapped)
        coarse = mixed.astype(BF16)
        fine = (mixed - coarse.astype(F32)).astype(BF16)
        term = fold(dot(coarse, wo[...]) + dot(fine, wo[...])).astype(BF16)
        out2[...] = term
        in2[z] = term

        @pl.loop(1, head_count)
        def _(n):
            send(1, out2, in2.at[z], {"head": (z + n) % head_count})

        await_bytes(in2.at[pl.ds(0, 7)], recv_sem.at[1])
        hidden = states + jnp.sum(in2[...].astype(F32), axis=0)
        hid[...] = hidden
        gain = jnp.where(upper, fg_ref[:, :512], fg_ref[:, 512:])
        normed = (hidden / jnp.sqrt(pair_mean(hidden) + EPS) * gain).astype(BF16)
        out3[...] = normed
        in3[mine] = normed

        @pl.loop(1, seq_count)
        def _(n):
            send(2, out3, in3.at[mine], {"seq": (me + n) % seq_count})

        await_bytes(in3.at[pl.ds(0, 23)], recv_sem.at[2])

    @pl.when(me % 4 == 3)
    def _():
        await_bytes(in3, recv_sem.at[2])

    rows = in3[...].astype(F32).reshape(192, 512).astype(BF16)
    routed = jnp.concatenate([dot(chl_sc[...], rows), dot(chr_sc[...], rows)], axis=1)
    routed = routed.astype(BF16)
    logits = dot_nt(routed, wr_sc[...])
    delta = jnp.sum(logits * eo_sc[...], axis=1, keepdims=True)
    gate = 1.0 / (1.0 + jnp.exp(-delta))
    for load in loads[6:9]:
        load.wait()
    downs = []
    for e in range(2):
        slots = routed[e * 16 : e * 16 + 16]
        gated = jax.nn.gelu(dot_nt(slots, wg[e]), approximate=True)
        units = (gated * dot_nt(slots, wu[e])).astype(BF16)
        downs.append(dot(units, wd[e]))
    down = (jnp.concatenate(downs, axis=0) * gate).astype(BF16)
    spread = dot(cbl_sc[...], down[:, :512]) + dot(cbr_sc[...], down[:, 512:])
    out4[...] = spread.reshape(24, 8, 512).astype(BF16)

    @pl.loop(1, seq_count)
    def _(n):
        target = (me + n) % seq_count

        @pl.when(target % 4 != 3)
        def _():
            request = (target // 4) * 3 + target % 4
            send(3, out4.at[request], in4.at[n], {"seq": target})

    @pl.when(owner)
    def _():
        in4[0] = out4[mine]
        await_bytes(in4.at[pl.ds(0, 31)], recv_sem.at[3])
        mix = jnp.sum(in4[...].astype(F32), axis=0)

        @pl.when(z != home)
        def _():
            out5[...] = mix.astype(BF16)
            send(4, out5, in5.at[z], {"head": home})

        @pl.when(z == home)
        def _():
            in5[z] = mix.astype(BF16)
            await_bytes(in5.at[pl.ds(0, 7)], recv_sem.at[4])
            final = (hid[...] + jnp.sum(in5[...].astype(F32), axis=0)).astype(BF16)
            out6[...] = final
            in6[me % 4] = final

            @pl.loop(1, seq_count)
            def _(n):
                target = {"seq": (me + n) % seq_count}
                send(5, out6, in6.at[me % 4], target, fin_sem.at[me % 4])

    loads[9].wait()
    for k in range(3):

        @pl.when(me != z * 4 + k)
        def _():
            await_bytes(in6.at[k], fin_sem.at[k])

    rows = in6[...].astype(F32)
    total = jnp.sum(rows * rows, axis=2, keepdims=True)
    total = total + jnp.concatenate([total[:, 4:8], total[:, 0:4]], axis=1)
    root = jnp.sqrt(total / 1024.0 + EPS)
    gain = jnp.where(upper, og_ref[:, :512], og_ref[:, 512:])
    scaled = (rows / root * gain[None]).reshape(24, 512).astype(BF16)
    left = dot_nt(scaled, voc[:, :512])
    right = dot_nt(scaled, voc[:, 512:])
    width = voc.shape[0]
    left = left.reshape(3, 8, width)[:, 0:4]
    right = right.reshape(3, 8, width)[:, 4:8]
    best = jnp.max(left + right, axis=2, keepdims=True)
    token = iota((3, 4, 128), 0) * 4 + iota((3, 4, 128), 1)
    place = iota((3, 4, 128), 2) == token
    best = jnp.sum(jnp.sum(jnp.where(place, best, 0.0), axis=0), axis=0, keepdims=True)
    out7[...] = best
    in7[0] = best

    @pl.loop(1, seq_count)
    def _(n):
        send(6, out7, in7.at[n], {"seq": (me + n) % seq_count})

    roots = jnp.sum(jnp.sum(jnp.where(place, root[:, 0:4], 0.0), axis=0), axis=0, keepdims=True)
    halves = [jnp.concatenate([rows[k, 0:4], rows[k, 4:8]], axis=1) for k in range(3)]
    fin_ref[...] = jnp.concatenate(halves, axis=0).astype(BF16)

    @pl.when(owner)
    def _():
        await_bytes(part_sc.at[pl.ds(0, 23)], send_sem.at[0])
        await_bytes(in2.at[pl.ds(0, 7)], send_sem.at[1])
        await_bytes(in4.at[pl.ds(0, 31)], send_sem.at[2])
        await_bytes(out4.at[pl.ds(0, 23)], send_sem.at[3])

        @pl.when(z != home)
        def _():
            await_bytes(out5, send_sem.at[4])

        @pl.when(z == home)
        def _():
            await_bytes(in4.at[pl.ds(0, 31)], send_sem.at[5])

    @pl.when(me % 4 == 3)
    def _():
        await_bytes(part_sc, send_sem.at[0])
        await_bytes(out4, send_sem.at[3])

    await_bytes(in7.at[pl.ds(0, 31)], recv_sem.at[6])
    best = jnp.max(in7[...], axis=0)
    stat_ref[...] = jnp.where(iota((8, 128), 0) == 0, roots, best)
    await_bytes(in7.at[pl.ds(0, 31)], send_sem.at[6])


def deliver_kernel(rows_ref, stat_ref, fin_ref, root_ref, best_ref):
    fin_ref[...] = rows_ref[...]
    root_ref[...] = stat_ref[0, 0:12]
    best_ref[...] = stat_ref[1, 0:12]


def shards(
    new_states,
    lengths,
    cache_keys,
    cache_values,
    buckets,
    attn_gain,
    w_query,
    w_key,
    w_value,
    rel_bias,
    w_out,
    ffn_gain,
    w_router,
    w_gate,
    w_up,
    w_down,
    expert_picks,
    final_gain,
    w_vocab,
):
    whole = pl.BlockSpec(memory_space=pltpu.VMEM)
    smem = pl.BlockSpec(memory_space=pltpu.SMEM)
    anywhere = pl.BlockSpec(memory_space=pl.ANY)
    small = (
        attn_gain[None],
        rel_bias.T,
        jnp.transpose(expert_picks, (0, 2, 1)),
        ffn_gain[None],
        w_router.T,
        final_gain[None],
    )
    large = (
        new_states,
        w_query,
        w_key,
        w_value,
        cache_keys,
        cache_values,
        buckets,
        w_out,
        jnp.transpose(w_gate, (0, 2, 1)),
        jnp.transpose(w_up, (0, 2, 1)),
        w_down,
        w_vocab.T,
    )
    tables = [((32, 192), BF16)] * 2 + [((192, 32), BF16)] * 2 + [((32, 32), F32), ((32, 1024), BF16)]
    staging = [
        ((24, 8, 128), F32),
        ((32, 8, 128), F32),
        ((8, 512), BF16),
        ((8, 8, 512), BF16),
        ((8, 512), BF16),
        ((24, 8, 512), BF16),
        ((24, 8, 512), BF16),
        ((32, 8, 512), BF16),
        ((8, 512), BF16),
        ((8, 8, 512), BF16),
        ((8, 512), BF16),
        ((3, 8, 512), BF16),
        ((1, 128), F32),
        ((32, 1, 128), F32),
        ((8, 512), F32),
    ]
    per = 6
    chunks = cache_keys.shape[0] // per
    rows, stats = pl.pallas_call(
        functools.partial(layer_kernel, per),
        out_shape=(
            jax.ShapeDtypeStruct((12, 1024), BF16),
            jax.ShapeDtypeStruct((8, 128), F32),
        ),
        in_specs=[smem] + [whole] * len(small) + [anywhere] * len(large),
        out_specs=(whole, whole),
        scratch_shapes=[pltpu.VMEM(a.shape, a.dtype) for a in large]
        + [pltpu.VMEM((24, 8, 128), F32)] * 3
        + [pltpu.VMEM((8, 128), F32)]
        + [pltpu.VMEM(s, t) for s, t in tables + staging]
        + [
            pltpu.SemaphoreType.DMA((10,)),
            pltpu.SemaphoreType.DMA((chunks,)),
            pltpu.SemaphoreType.DMA((chunks,)),
            pltpu.SemaphoreType.DMA((7,)),
            pltpu.SemaphoreType.DMA((7,)),
            pltpu.SemaphoreType.DMA((3,)),
        ],
        compiler_params=pltpu.CompilerParams(collective_id=0, has_side_effects=True),
        name="layer",
    )(lengths, *small, *large)
    return pl.pallas_call(
        deliver_kernel,
        out_shape=(
            jax.ShapeDtypeStruct((12, 1024), BF16),
            jax.ShapeDtypeStruct((12,), F32),
            jax.ShapeDtypeStruct((12,), F32),
        ),
        in_specs=[whole] * 2,
        out_specs=(whole,) * 3,
        name="deliver",
    )(rows, stats)


def solution(mesh):
    placed = (
        P(),
        P(),
        P(None, "seq", "head"),
        P(None, "seq", "head"),
        P(None, None, "seq"),
        P(),
        P(None, "head"),
        P(None, "head"),
        P(None, "head"),
        P(None, "head"),
        P("head", None),
        P(),
        P(),
        P("head", None, "seq"),
        P("head", None, "seq"),
        P("head", "seq", None),
        P(),
        P(),
        P(None, "seq"),
    )
    return jax.shard_map(
        shards,
        mesh=mesh,
        in_specs=placed,
        out_specs=(P("head", None), P("head"), P("head")),
        check_vma=False,
    )
```

```python
import functools

import jax
import jax.numpy as jnp
from jax import lax
from jax.experimental import pallas as pl
from jax.experimental.pallas import tpu as pltpu
from jax.sharding import PartitionSpec as P

F32 = jnp.float32
BF16 = jnp.bfloat16
CAP = 4
EPS = 1e-06
LOW = -1e30
MESH = pl.DeviceIdType.MESH
NT = (((1,), (1,)), ((), ()))
HIGH = lax.Precision.HIGHEST


def owner_of(request):
    return (request // 3 + 3 * (request % 3)) % 8 * 4 + request % 3


def request_of(position):
    return (position // 4 + 5 * (position % 4)) % 8 * 3 + position % 4


def iota(shape, dim):
    return lax.broadcasted_iota(jnp.int32, shape, dim)


def dot(a, b):
    return jnp.dot(a, b, preferred_element_type=F32)


def dot_nt(a, b, precision=None):
    return lax.dot_general(a, b, NT, precision=precision, preferred_element_type=F32)


def layer_kernel(
    per,
    len_hbm,
    ag_hbm,
    rb_hbm,
    pk_hbm,
    fg_hbm,
    wr_hbm,
    og_hbm,
    x_hbm,
    wq_hbm,
    wk_hbm,
    wv_hbm,
    k_hbm,
    v_hbm,
    b_hbm,
    wo_hbm,
    wg_hbm,
    wu_hbm,
    wd_hbm,
    voc_hbm,
    fin_ref,
    stat_ref,
    len_sc,
    ag_ref,
    rb_ref,
    pk_ref,
    fg_ref,
    wr_ref,
    og_ref,
    xb,
    wq,
    wk,
    wv,
    kb,
    vb,
    bb,
    wo,
    wg,
    wu,
    wd,
    voc,
    q_sc,
    kn_sc,
    vn_sc,
    tb_sc,
    chl_sc,
    chr_sc,
    cbl_sc,
    cbr_sc,
    eo_sc,
    wr_sc,
    part_sc,
    in1,
    out2,
    in2,
    out3,
    in3,
    out4,
    in4,
    out5,
    in5,
    out6,
    in6,
    out7,
    in7,
    hid,
    small_sem,
    load_sem,
    k_sem,
    v_sem,
    send_sem,
    recv_sem,
    fin_sem,
):
    seq_count, head_count = 32, 8
    far = [0, 1, 2, 1]
    steps = [(dx, dy, dc) for dx in range(4) for dy in range(4) for dc in range(2)]
    steps = sorted(steps[1:], key=lambda d: (-far[d[0]] - far[d[1]], d))
    turns = [4, 3, 5, 2, 6, 1, 7]
    me = lax.axis_index("seq")
    z = lax.axis_index("head")
    owner = me % 4 != 3
    home = (me // 4 + 5 * (me % 4)) % 8
    mine = home * 3 + me % 4
    across = [(me // 8 + d) % 4 * 8 for d in range(4)]
    along = [(me // 2 + d) % 4 * 2 for d in range(4)]
    side = [(me + d) % 2 for d in range(2)]
    peers = [(n + 1, across[dx] + along[dy] + side[dc]) for n, (dx, dy, dc) in enumerate(steps)]
    rings = [(z + n) % head_count for n in turns]
    requests, span = kb.shape[0], kb.shape[1]
    chunks = requests // per

    def cache_load(src, dst, sem, c):
        rows = pl.ds(c * per, per)
        return pltpu.make_async_copy(src.at[rows], dst.at[rows], sem.at[c])

    pairs = [
        (pk_hbm, pk_ref),
        (wr_hbm, wr_ref),
        (rb_hbm, rb_ref),
        (ag_hbm, ag_ref),
        (len_hbm, len_sc),
        (fg_hbm, fg_ref),
        (og_hbm, og_ref),
    ]
    smalls = [
        pltpu.make_async_copy(src, dst, small_sem.at[n]) for n, (src, dst) in enumerate(pairs)
    ]
    for load in smalls:
        load.start()
    first = [(x_hbm, xb), (wq_hbm, wq), (wk_hbm, wk), (wv_hbm, wv), (b_hbm, bb)]
    later = [(wo_hbm, wo), (wg_hbm, wg), (wu_hbm, wu), (wd_hbm, wd), (voc_hbm, voc)]
    loads = [
        pltpu.make_async_copy(src, dst, load_sem.at[n]) for n, (src, dst) in enumerate(first + later)
    ]
    for load in loads[:5]:
        load.start()
    for c in range(chunks):
        cache_load(k_hbm, kb, k_sem, c).start()
        cache_load(v_hbm, vb, v_sem, c).start()
    for load in loads[5:]:
        load.start()

    barrier = pltpu.get_barrier_semaphore()

    for _, peer in peers:
        pl.semaphore_signal(barrier, inc=1, device_id={"seq": peer}, device_id_type=MESH)
    for ring in rings:
        pl.semaphore_signal(barrier, inc=1, device_id={"head": ring}, device_id_type=MESH)

    def send(stage, src, dst, target, sem=None):
        pltpu.make_async_remote_copy(
            src_ref=src,
            dst_ref=dst,
            send_sem=send_sem.at[stage],
            recv_sem=recv_sem.at[stage] if sem is None else sem,
            device_id=target,
            device_id_type=MESH,
        ).start()

    def await_bytes(ref, sem):
        pltpu.make_async_copy(ref, ref, sem).wait()

    for load in smalls:
        load.wait()

    i = iota((32, 24), 0)
    e, t, c = z * 2 + i // 16, (i // 4) % 4, i % 4
    p0 = jnp.zeros((32, 24), jnp.int32)
    p1 = jnp.zeros((32, 24), jnp.int32)
    for s in range(4):
        p0 = jnp.where(t == s, pk_ref[s, 0:1, :], p0)
        p1 = jnp.where(t == s, pk_ref[s, 1:2, :], p1)
    inc = jnp.where((p0 == e) | (p1 == e), 1.0, 0.0)
    before = jnp.where(iota((24, 24), 0) < iota((24, 24), 1), 1.0, 0.0)
    before = dot(inc.astype(BF16), before.astype(BF16))
    ch = jnp.where(before == c.astype(F32), inc, 0.0)
    other = jnp.sum(ch * (p0 + p1 - e).astype(F32), axis=1, keepdims=True)
    n = iota((32, 32), 1) % 16
    e16 = z * 2 + iota((32, 32), 0) // 16
    eo_sc[...] = jnp.where(n == e16, 1.0, 0.0) - jnp.where(n.astype(F32) == other, 1.0, 0.0)
    ch = ch.astype(BF16)
    grow = jnp.where(iota((24, 192), 1) // 8 == iota((24, 192), 0), 1.0, 0.0).astype(BF16)
    wide = dot(ch, grow)
    l8, t_r = iota((32, 192), 1) % 8, (iota((32, 192), 0) // 4) % 4
    chl_sc[...] = jnp.where(l8 == t_r, wide, 0.0).astype(BF16)
    chr_sc[...] = jnp.where(l8 == t_r + 4, wide, 0.0).astype(BF16)
    grow_t = jnp.where(iota((192, 24), 0) // 8 == iota((192, 24), 1), 1.0, 0.0).astype(BF16)
    tall = dot_nt(grow_t, ch)
    r8, t_l = iota((192, 32), 0) % 8, (iota((192, 32), 1) // 4) % 4
    cbl_sc[...] = jnp.where(r8 == t_l, tall, 0.0).astype(BF16)
    cbr_sc[...] = jnp.where(r8 == t_l + 4, tall, 0.0).astype(BF16)
    router = wr_ref[...]
    coarse = router.astype(BF16)
    wr_sc[0:16] = coarse
    wr_sc[16:32] = (router - coarse.astype(F32)).astype(BF16)
    tb_sc[...] = jnp.zeros((8, 128), F32)
    tb_sc[:, 0:32] = jnp.where(iota((8, 32), 0) < 4, rb_ref[0:1, :], rb_ref[1:2, :])

    for load in loads[:4]:
        load.wait()
    x = xb[...].astype(F32)
    root = jnp.sqrt(jnp.mean(x * x, axis=-1, keepdims=True) + EPS)
    scaled = (x / root * ag_ref[...]).astype(BF16)
    i, j = iota((192, 96), 0), iota((192, 96), 1)
    spread = jnp.where(j == (i // 8) * 4 + i % 4, 1.0, 0.0).astype(BF16)
    front = iota((192, 128), 0) % 8 < 4
    q = dot(spread, dot(scaled, wq[...]).astype(BF16))
    q = jnp.where((iota((192, 128), 1) < 64) == front, q, 0.0)
    q_sc[...] = q.reshape(24, 8, 128)
    kn_sc[...] = dot(spread, dot(scaled, wk[...]).astype(BF16)).reshape(24, 8, 128)
    v = dot(spread, dot(scaled, wv[...]).astype(BF16))
    vn_sc[...] = jnp.where(front, v, 0.0).reshape(24, 8, 128)

    loads[4].wait()
    pl.semaphore_wait(barrier, seq_count + head_count - 2)

    row8, lane8 = iota((8, 128), 0), iota((8, 128), 1)
    own = (lane8 < 64) == (row8 < 4)
    low_lane = lane8 % 64 < 32
    wide_pos = iota((8, span), 1) + me * span
    table = tb_sc[...]

    @pl.loop(0, chunks)
    def _(c):
        cache_load(k_hbm, kb, k_sem, c).wait()
        cache_load(v_hbm, vb, v_sem, c).wait()
        group = [c * per + i for i in range(per)]
        scores = [dot_nt(q_sc[r].astype(BF16), kb[r]) for r in group]
        valid = [wide_pos < len_sc[r] for r in group]
        marks = [bb[r] for r in group]
        marks = [jnp.concatenate([b, b], axis=0) for b in marks]
        bias = [
            jnp.concatenate(
                [
                    jnp.take_along_axis(
                        table, b[:, p : p + 128], axis=1, mode="promise_in_bounds"
                    )
                    for p in range(0, span, 128)
                ],
                axis=1,
            )
            for b in marks
        ]
        scores = [jnp.where(ok, a + b, LOW) for ok, a, b in zip(valid, scores, bias)]
        tops = [jnp.max(a, axis=1, keepdims=True) for a in scores]
        weights = [
            jnp.where(ok, jnp.exp(a - top), 0.0) for ok, a, top in zip(valid, scores, tops)
        ]
        summed = [dot(w.astype(BF16), vb[r]) for w, r in zip(weights, group)]
        masses = [jnp.sum(w, axis=1, keepdims=True) for w in weights]
        for r, top, mass, total in zip(group, tops, masses, summed):
            part_sc[r] = jnp.where(own, total, jnp.where(low_lane, top, mass))
        for r in group:
            target = owner_of(r)

            @pl.when(target != me)
            def _():
                slot = (target - me + seq_count) % seq_count
                send(0, part_sc.at[r], in1.at[slot], {"seq": target})

    upper = iota((8, 512), 0) < 4

    def fold(rows):
        return jnp.where(upper, rows[:, :512], rows[:, 512:])

    def pair_mean(values):
        total = jnp.sum(values * values, axis=1, keepdims=True)
        return (total + jnp.concatenate([total[4:8], total[0:4]], axis=0)) / 1024.0

    loads[5].wait()

    @pl.when(owner)
    def _():
        in1[0] = part_sc[mine]
        q8 = q_sc[mine].astype(BF16)
        gap = iota((8, 8), 0) % 4 - iota((8, 8), 1)
        fresh = dot_nt(q8, kn_sc[mine].astype(BF16))
        for d in range(4):
            fresh = fresh + jnp.where(gap == d, table[:, d : d + 1], 0.0)
        known = gap >= 0
        top = jnp.max(jnp.where(known, fresh, LOW), axis=1, keepdims=True)
        weights = jnp.where(known, jnp.exp(fresh - top), 0.0)
        mass = jnp.sum(weights, axis=1, keepdims=True)
        total = dot(weights.astype(BF16), vn_sc[mine].astype(BF16))
        in1[32] = jnp.where(own, total, jnp.where(low_lane, top, mass))
        i, j = iota((8, 96), 0), iota((8, 96), 1)
        pick = jnp.where(j == mine * 4 + i % 4, 1.0, 0.0).astype(BF16)
        states = fold(dot(pick, xb[...]))
        await_bytes(in1.at[pl.ds(0, 31)], recv_sem.at[0])
        part = in1[...]
        r3, l3 = iota((33, 8, 128), 1), iota((33, 8, 128), 2)
        spare = (l3 < 64) != (r3 < 4)
        tops = jnp.max(jnp.where(spare & (l3 % 64 < 32), part, -3e38), axis=2, keepdims=True)
        masses = jnp.max(jnp.where(spare & (l3 % 64 >= 32), part, -3e38), axis=2, keepdims=True)
        lead = jnp.exp(tops - jnp.max(tops, axis=0, keepdims=True))
        mass = jnp.sum(masses * lead, axis=0)
        both = jnp.sum(part * lead, axis=0) / mass
        swapped = jnp.concatenate([both[4:8], both[0:4]], axis=0)
        mixed = jnp.where(own, both, swapped)
        coarse = mixed.astype(BF16)
        fine = (mixed - coarse.astype(F32)).astype(BF16)
        term = fold(dot(coarse, wo[...]) + dot(fine, wo[...])).astype(BF16)
        out2[...] = term
        in2[z] = term

        for ring in rings:
            send(1, out2, in2.at[z], {"head": ring})

        await_bytes(in2.at[pl.ds(0, 7)], recv_sem.at[1])
        hidden = states + jnp.sum(in2[...].astype(F32), axis=0)
        hid[...] = hidden
        gain = jnp.where(upper, fg_ref[:, :512], fg_ref[:, 512:])
        normed = (hidden / jnp.sqrt(pair_mean(hidden) + EPS) * gain).astype(BF16)
        out3[...] = normed
        in3[mine] = normed

        for _, peer in peers:
            send(2, out3, in3.at[mine], {"seq": peer})

        await_bytes(in3.at[pl.ds(0, 23)], recv_sem.at[2])

    @pl.when(me % 4 == 3)
    def _():
        await_bytes(in3, recv_sem.at[2])

    rows = in3[...].astype(F32).reshape(192, 512).astype(BF16)
    routed = jnp.concatenate([dot(chl_sc[...], rows), dot(chr_sc[...], rows)], axis=1)
    routed = routed.astype(BF16)
    logits = dot_nt(routed, wr_sc[...])
    delta = jnp.sum(logits * eo_sc[...], axis=1, keepdims=True)
    gate = 1.0 / (1.0 + jnp.exp(-delta))
    for load in loads[6:9]:
        load.wait()
    downs = []
    for e in range(2):
        slots = routed[e * 16 : e * 16 + 16]
        gated = jax.nn.gelu(dot_nt(slots, wg[e]), approximate=True)
        units = (gated * dot_nt(slots, wu[e])).astype(BF16)
        downs.append(dot(units, wd[e]))
    down = (jnp.concatenate(downs, axis=0) * gate).astype(BF16)
    spread = dot(cbl_sc[...], down[:, :512]) + dot(cbr_sc[...], down[:, 512:])
    out4[...] = spread.reshape(24, 8, 512).astype(BF16)

    for n, peer in peers:

        @pl.when(peer % 4 != 3)
        def _():
            send(3, out4.at[request_of(peer)], in4.at[n], {"seq": peer})

    @pl.when(owner)
    def _():
        in4[0] = out4[mine]
        await_bytes(in4.at[pl.ds(0, 31)], recv_sem.at[3])
        mix = jnp.sum(in4[...].astype(F32), axis=0)

        @pl.when(z != home)
        def _():
            out5[...] = mix.astype(BF16)
            send(4, out5, in5.at[z], {"head": home})

        @pl.when(z == home)
        def _():
            in5[z] = mix.astype(BF16)
            await_bytes(in5.at[pl.ds(0, 7)], recv_sem.at[4])
            final = (hid[...] + jnp.sum(in5[...].astype(F32), axis=0)).astype(BF16)
            out6[...] = final
            in6[me % 4] = final

            for _, peer in peers:
                send(5, out6, in6.at[me % 4], {"seq": peer}, fin_sem.at[me % 4])

    loads[9].wait()
    for k in range(3):

        @pl.when(me != owner_of(z * 3 + k))
        def _():
            await_bytes(in6.at[k], fin_sem.at[k])

    rows = in6[...].astype(F32)
    total = jnp.sum(rows * rows, axis=2, keepdims=True)
    total = total + jnp.concatenate([total[:, 4:8], total[:, 0:4]], axis=1)
    root = jnp.sqrt(total / 1024.0 + EPS)
    gain = jnp.where(upper, og_ref[:, :512], og_ref[:, 512:])
    scaled = (rows / root * gain[None]).reshape(24, 512).astype(BF16)
    left = dot_nt(scaled, voc[:, :512])
    right = dot_nt(scaled, voc[:, 512:])
    width = voc.shape[0]
    left = left.reshape(3, 8, width)[:, 0:4]
    right = right.reshape(3, 8, width)[:, 4:8]
    best = jnp.max(left + right, axis=2, keepdims=True)
    token = iota((3, 4, 128), 0) * 4 + iota((3, 4, 128), 1)
    place = iota((3, 4, 128), 2) == token
    best = jnp.sum(jnp.sum(jnp.where(place, best, 0.0), axis=0), axis=0, keepdims=True)
    out7[...] = best
    in7[0] = best

    for n, peer in peers:
        send(6, out7, in7.at[n], {"seq": peer})

    roots = jnp.sum(jnp.sum(jnp.where(place, root[:, 0:4], 0.0), axis=0), axis=0, keepdims=True)
    halves = [jnp.concatenate([rows[k, 0:4], rows[k, 4:8]], axis=1) for k in range(3)]
    fin_ref[...] = jnp.concatenate(halves, axis=0).astype(BF16)

    @pl.when(owner)
    def _():
        await_bytes(part_sc.at[pl.ds(0, 23)], send_sem.at[0])
        await_bytes(in2.at[pl.ds(0, 7)], send_sem.at[1])
        await_bytes(in4.at[pl.ds(0, 31)], send_sem.at[2])
        await_bytes(out4.at[pl.ds(0, 23)], send_sem.at[3])

        @pl.when(z != home)
        def _():
            await_bytes(out5, send_sem.at[4])

        @pl.when(z == home)
        def _():
            await_bytes(in4.at[pl.ds(0, 31)], send_sem.at[5])

    @pl.when(me % 4 == 3)
    def _():
        await_bytes(part_sc, send_sem.at[0])
        await_bytes(out4, send_sem.at[3])

    await_bytes(in7.at[pl.ds(0, 31)], recv_sem.at[6])
    best = jnp.max(in7[...], axis=0)
    stat_ref[...] = jnp.where(iota((8, 128), 0) == 0, roots, best)
    await_bytes(in7.at[pl.ds(0, 31)], send_sem.at[6])


def deliver_kernel(rows_ref, stat_ref, fin_ref, root_ref, best_ref):
    fin_ref[...] = rows_ref[...]
    root_ref[...] = stat_ref[0, 0:12]
    best_ref[...] = stat_ref[1, 0:12]


def shards(
    new_states,
    lengths,
    cache_keys,
    cache_values,
    buckets,
    attn_gain,
    w_query,
    w_key,
    w_value,
    rel_bias,
    w_out,
    ffn_gain,
    w_router,
    w_gate,
    w_up,
    w_down,
    expert_picks,
    final_gain,
    w_vocab,
):
    whole = pl.BlockSpec(memory_space=pltpu.VMEM)
    anywhere = pl.BlockSpec(memory_space=pl.ANY)
    small = (
        attn_gain[None],
        rel_bias.T,
        jnp.transpose(expert_picks, (0, 2, 1)),
        ffn_gain[None],
        w_router.T,
        final_gain[None],
    )
    large = (
        new_states,
        w_query,
        w_key,
        w_value,
        cache_keys,
        cache_values,
        buckets,
        w_out,
        jnp.transpose(w_gate, (0, 2, 1)),
        jnp.transpose(w_up, (0, 2, 1)),
        w_down,
        w_vocab.T,
    )
    tables = [((32, 192), BF16)] * 2 + [((192, 32), BF16)] * 2 + [((32, 32), F32), ((32, 1024), BF16)]
    staging = [
        ((24, 8, 128), F32),
        ((33, 8, 128), F32),
        ((8, 512), BF16),
        ((8, 8, 512), BF16),
        ((8, 512), BF16),
        ((24, 8, 512), BF16),
        ((24, 8, 512), BF16),
        ((32, 8, 512), BF16),
        ((8, 512), BF16),
        ((8, 8, 512), BF16),
        ((8, 512), BF16),
        ((3, 8, 512), BF16),
        ((1, 128), F32),
        ((32, 1, 128), F32),
        ((8, 512), F32),
    ]
    per = 6
    chunks = cache_keys.shape[0] // per
    rows, stats = pl.pallas_call(
        functools.partial(layer_kernel, per),
        out_shape=(
            jax.ShapeDtypeStruct((12, 1024), BF16),
            jax.ShapeDtypeStruct((8, 128), F32),
        ),
        in_specs=[anywhere] * (1 + len(small) + len(large)),
        out_specs=(whole, whole),
        scratch_shapes=[pltpu.SMEM(lengths.shape, lengths.dtype)]
        + [pltpu.VMEM(a.shape, a.dtype) for a in small + large]
        + [pltpu.VMEM((24, 8, 128), F32)] * 3
        + [pltpu.VMEM((8, 128), F32)]
        + [pltpu.VMEM(s, t) for s, t in tables + staging]
        + [
            pltpu.SemaphoreType.DMA((7,)),
            pltpu.SemaphoreType.DMA((10,)),
            pltpu.SemaphoreType.DMA((chunks,)),
            pltpu.SemaphoreType.DMA((chunks,)),
            pltpu.SemaphoreType.DMA((7,)),
            pltpu.SemaphoreType.DMA((7,)),
            pltpu.SemaphoreType.DMA((3,)),
        ],
        compiler_params=pltpu.CompilerParams(collective_id=0, has_side_effects=True),
        name="layer",
    )(lengths, *small, *large)
    return pl.pallas_call(
        deliver_kernel,
        out_shape=(
            jax.ShapeDtypeStruct((12, 1024), BF16),
            jax.ShapeDtypeStruct((12,), F32),
            jax.ShapeDtypeStruct((12,), F32),
        ),
        in_specs=[whole] * 2,
        out_specs=(whole,) * 3,
        name="deliver",
    )(rows, stats)


def solution(mesh):
    placed = (
        P(),
        P(),
        P(None, "seq", "head"),
        P(None, "seq", "head"),
        P(None, None, "seq"),
        P(),
        P(None, "head"),
        P(None, "head"),
        P(None, "head"),
        P(None, "head"),
        P("head", None),
        P(),
        P(),
        P("head", None, "seq"),
        P("head", None, "seq"),
        P("head", "seq", None),
        P(),
        P(),
        P(None, "seq"),
    )
    return jax.shard_map(
        shards,
        mesh=mesh,
        in_specs=placed,
        out_specs=(P("head", None), P("head"), P("head")),
        check_vma=False,
    )
```
